128 devices in a mesh: grp: 4 (over x), dev: 32 (over y, z, core).
Axes of the slice: x: 4, y: 4, z: 4, core: 2. Of those that a mesh axis runs over, the one named last changes fastest.
Arguments:
- basis: float32 [2048, 64, 1024], P(('grp', 'dev')), may hold values from -0.25 to 0.25
- leaf_transfer: float32 [2048, 4096], P(('grp', 'dev')), may hold values from -0.75 to 1.75, as said below
- upper_transfer: float32 [1024, 4096], P(('grp', 'dev')), may hold values from -0.75 to 1.75, as said below
- coupling: float32 [16384, 4096], P(('grp', 'dev')), may hold values from -6 to 6
- row_leaf: int32 [16384], P(('grp', 'dev')), may hold values from 0 to 15
- col_dev: int32 [16384, 1], P(('grp', 'dev')), may hold values from 0 to 127; in each aligned block of 128 rows (0 to 127, 128 to 255, ...) at most 2 rows name the same one
- col_leaf: int32 [16384], P(('grp', 'dev')), may hold values from 0 to 15
Outputs:
- ortho_basis: float32 [2048, 64, 1024], P(('grp', 'dev'))
- leaf_transfer_out: float32 [2048, 4096], P(('grp', 'dev'))
- upper_transfer_out: float32 [1024, 4096], P(('grp', 'dev'))
- coupling_out: float32 [16384, 4096], P(('grp', 'dev'))
The draws below stay inside these ranges and needn't reach their ends.
Inputs may be any that keep to these rules, and one draw needn't show every extreme that they name: `col_dev`: among the 128 blocks of one device no device index appears more than 2 times, and some index appears exactly 2 times on some device. `leaf_transfer`: each row is a K x K matrix near the identity. `upper_transfer`: each row is a K x K matrix near the identity.
All inputs are finite; a program needn't handle non-finite values.
Results may differ from the reference program's by a relative error of at most 0.0003.
Values sent between devices are 32-bit elements; how exact they have to be, the bound alone decides.
No kernel may reach another device: no remote copies, remote signals or barrier semaphores. Data moves between devices by JAX's collectives and lax.ppermute only.
A program may use at most 128 MiB of HBM per device.

```python
import math
import jax
import jax.numpy as jnp
import numpy as np
from jax import lax

K = 64
LEAF = 1024
LEAF_DEV = 16
BLK_DEV = 128
NLEAF = 2048
NL1 = 1024
SPAN = 256
NBLK = 16384
CAP = 2
DEVICES = 128


def near_identity(key, count, width, salt):
    noise_key = jax.random.fold_in(key, salt)
    noise = jnp.clip(jax.random.normal(noise_key, (count, width, width), jnp.float32), -6.0, 6.0)
    spread = 0.5 / width ** 0.5
    mats = jnp.eye(width, dtype=jnp.float32)[None] + spread * noise
    return mats.reshape(count, width * width)


def draw_leaf_transfer(key, part):
    return near_identity(key, NLEAF, K, 11)


def draw_upper_transfer(key, part):
    return near_identity(key, NL1, K, 23)


def touch_ends(array, stream_key, smallest, top_value):
    index_at = [jax.random.randint(jax.random.fold_in(stream_key, axis), (), 0, length) for axis, length in enumerate(array.shape)]
    widest = array.shape.index(max(array.shape))
    next_to = index_at[:widest] + [(index_at[widest] + 1) % array.shape[widest]] + index_at[widest + 1:]
    return array.at[tuple(index_at)].set(smallest).at[tuple(next_to)].set(top_value)


def block_levels(own_key, shape, pieces, low, top_value):
    def one(position, parts):
        draws = jax.random.uniform(jax.random.fold_in(jax.random.fold_in(own_key, 6), position), (parts,), jnp.float32, low / len(pieces), top_value / len(pieces))
        return jnp.repeat(jnp.exp(draws), shape[position] // parts).reshape((-1,) + (1,) * (len(shape) - position - 1))

    level = one(*pieces[0])
    for cut in pieces[1:]:
        level = level * one(*cut)
    return level


def routed_block(rng, own, number, rows, count, top, limit, skew):
    sequence = jax.random.permutation(rng, count)
    heavy_load, common = portions_of(count, rows * top, limit, skew, True), portions_of(count, rows * top, limit, skew, False)
    places = jnp.arange(count)

    def named(lengths, turn):
        used = int((lengths > 0).sum())
        fixed = max(1, used // 4)
        moved = fixed + (places - fixed + turn * (used - fixed)) % max(1, count - fixed)
        return jnp.zeros((count,), jnp.int32).at[sequence[jnp.where(places < fixed, places, moved)]].set(jnp.asarray(lengths, jnp.int32))

    lengths = jnp.where(number % 4 == 0, named(heavy_load, number // 4), named(common, number - number // 4 - 1))
    mixed = jax.random.permutation(jax.random.fold_in(own, 3), count)
    giver, taker = mixed[0:count // 2 * 2:2], mixed[1:count // 2 * 2:2]
    slack = jnp.minimum(lengths[giver] - 1, limit - lengths[taker]) // 2
    slack = jnp.where((giver == sequence[0]) | (taker == sequence[0]) | (lengths[taker] == 0), 0, jnp.maximum(slack, 0))
    moved = jax.random.randint(jax.random.fold_in(own, 4), (count // 2,), 0, 1 << 20) % (slack + 1)
    lengths = lengths.at[giver].add(-moved).at[taker].add(moved)
    members = jnp.searchsorted(jnp.cumsum(lengths), jnp.arange(rows * top), side="right").astype(jnp.int32)
    listing = members.reshape(top, rows).T
    listing = listing[jax.random.permutation(jax.random.fold_in(own, 1), rows)]
    turn = jax.random.randint(jax.random.fold_in(own, 2), (rows, 1), 0, top)
    return jnp.take_along_axis(listing, (jnp.arange(top)[None, :] + turn) % top, axis=1)


def portions_of(count, total, bound, skew, full):
    weights = [(1 << 20) // math.isqrt(standing ** skew) + 1 for standing in range(1, count + 1)]
    largest = bound if full else min(bound, max(-(-total // count), total * weights[0] // sum(weights)))
    least = 1 if total - largest >= count - 1 else 0
    given, rest = [largest] + [least] * (count - 1), total - largest - least * (count - 1)
    while rest > 0:
        candidates = [i for i in range(1, count) if given[i] < largest] or [i for i in range(1, count) if given[i] < bound]
        whole, remaining = sum([weights[i] for i in candidates]), rest
        for i in candidates:
            extra = min(bound - given[i], max(1, remaining * weights[i] // whole), rest)
            given[i] = given[i] + extra
            rest = rest - extra
    return np.array(given)


def scatter_about(key, extent, scale, limit, pieces=(), kind=jnp.bfloat16):
    gain = block_levels(key, extent, pieces, -0.22, 0.18) if pieces else 1.0
    drawn = jax.random.normal(key, extent, jnp.float32) * scale * gain
    return jnp.minimum(jnp.maximum(drawn, -limit), limit).astype(kind)


def setup_inputs(seed: int = 0) -> dict:
    splits = jax.random.split(jax.random.key(seed), 8)
    basis = scatter_about(splits[0], (NLEAF, K, LEAF), 0.03125, 0.25, ((0, 128),), jnp.float32)
    leaf_transfer = draw_leaf_transfer(jax.random.fold_in(splits[7], 71), 0)
    upper_transfer = draw_upper_transfer(jax.random.fold_in(splits[7], 71), 0)
    coupling = scatter_about(splits[3], (NBLK, K * K), 1.0, 6.0, ((0, 128),), jnp.float32)
    row_leaf = touch_ends(jax.random.randint(splits[4], (NBLK,), 0, LEAF_DEV), jax.random.fold_in(splits[4], 1), 0, LEAF_DEV - 1).astype(jnp.int32)
    col_dev_keys = jax.random.split(jax.random.fold_in(splits[5], 1), NBLK // BLK_DEV)
    col_dev_turns = jax.random.permutation(jax.random.fold_in(splits[5], 3), NBLK // BLK_DEV)
    col_dev = jax.vmap(lambda own, number: routed_block(jax.random.fold_in(splits[5], 2), own, number, BLK_DEV, DEVICES, 1, CAP, 2))(col_dev_keys, col_dev_turns).reshape((NBLK, 1))
    col_leaf = touch_ends(jax.random.randint(splits[6], (NBLK,), 0, LEAF_DEV), jax.random.fold_in(splits[6], 1), 0, LEAF_DEV - 1).astype(jnp.int32)
    return dict(basis=basis, leaf_transfer=leaf_transfer, upper_transfer=upper_transfer, coupling=coupling, row_leaf=row_leaf, col_dev=col_dev, col_leaf=col_leaf)


exact_mode = lax.Precision.HIGHEST

def left_solve(lower, mats):
    return lax.linalg.triangular_solve(lower, mats, left_side=True, lower=True)

def right_solve(lower, mats):
    return lax.linalg.triangular_solve(lower, mats, left_side=False, lower=True, transpose_a=True)

def transpose_mul(first, second):
    return jnp.einsum('nji,njk->nik', first, second, precision=exact_mode)

def reference(basis, leaf_transfer, upper_transfer, coupling, row_leaf, col_dev, col_leaf):
    leaves, width, points = basis.shape
    gram = jnp.einsum('nkp,njp->nkj', basis, basis, precision=exact_mode)
    lower = jnp.linalg.cholesky(gram)
    ortho_basis = left_solve(lower, basis) * math.sqrt(points)
    lifted = transpose_mul(lower, leaf_transfer.reshape(leaves, width, width))
    inner = transpose_mul(lifted, lifted)
    lower_one = jnp.linalg.cholesky(inner.reshape(leaves // 2, 2, width, width).sum(axis=1))
    new_leaf = right_solve(jnp.repeat(lower_one, 2, axis=0), lifted)
    clusters = leaves // 2
    raised = transpose_mul(lower_one, upper_transfer.reshape(clusters, width, width))
    inner_up = transpose_mul(raised, raised)
    summed = inner_up.reshape(clusters // (2 * SPAN), 2, SPAN, width, width).sum(axis=1)
    lower_two = jnp.linalg.cholesky(summed)
    lower_two = jnp.broadcast_to(lower_two[:, None], (clusters // (2 * SPAN), 2, SPAN, width, width)).reshape(clusters, width, width)
    new_upper = right_solve(lower_two, raised)
    owners = NBLK // BLK_DEV
    upper_leaf = jnp.swapaxes(lower, 1, 2)

    def one_owner(index):
        start = (index * BLK_DEV).astype(jnp.int32)
        blocks = lax.dynamic_slice_in_dim(coupling, start, BLK_DEV, 0).reshape(BLK_DEV, width, width)
        rows = lax.dynamic_slice_in_dim(row_leaf, start, BLK_DEV, 0) + index * LEAF_DEV
        dests = lax.dynamic_slice_in_dim(col_dev[:, 0], start, BLK_DEV, 0)
        cols = dests * LEAF_DEV + lax.dynamic_slice_in_dim(col_leaf, start, BLK_DEV, 0)
        row_factor = jnp.take(upper_leaf, rows.astype(jnp.int32), axis=0)
        col_factor = jnp.take(upper_leaf, cols.astype(jnp.int32), axis=0)
        left = jnp.einsum('bij,bjk->bik', row_factor, blocks, precision=exact_mode)
        done = jnp.einsum('bij,bkj->bik', left, col_factor, precision=exact_mode)
        return done.reshape(BLK_DEV, width * width)
    coupling_out = lax.map(one_owner, jnp.arange(owners, dtype=jnp.int32)).reshape(NBLK, width * width)
    return (ortho_basis, new_leaf.reshape(leaves, width * width), new_upper.reshape(clusters, width * width), coupling_out)
```

```python
import functools
import math

import jax
import jax.numpy as jnp
from jax import lax
from jax.experimental import pallas as pl
from jax.experimental.pallas import tpu as pltpu
from jax.sharding import PartitionSpec as P

BOTH = ("grp", "dev")
ROWS = 40
bf16, f32 = jnp.bfloat16, jnp.float32


def cost(flops, moved):
    return pl.CostEstimate(flops=int(flops), bytes_accessed=int(moved), transcendentals=0)


def halves(x):
    high = x.astype(bf16).astype(f32)
    return high, x - high


def left_triple(x):
    high, low = halves(x)
    return jnp.concatenate([high, high, low], axis=1).astype(bf16)


def right_triple(x):
    high, low = halves(x)
    return jnp.concatenate([high, low, high], axis=0).astype(bf16)


def product(first, second):
    return jnp.dot(left_triple(first), right_triple(second), preferred_element_type=f32)


def lanes(shape):
    return lax.broadcasted_iota(jnp.int32, shape, len(shape) - 1)


def sublanes(shape):
    return lax.broadcasted_iota(jnp.int32, shape, len(shape) - 2)


def with_identity(square):
    lane, row = lanes(square.shape), sublanes(square.shape)
    return jnp.where(lane < square.shape[0], square, (lane == row + square.shape[0]).astype(f32))


def eliminate(work, width, batch):
    lane = lanes((batch, 2 * width))
    for j in range(width):
        row = work[j * batch : (j + 1) * batch, :]
        pivot = row[:, j : j + 1]
        if j + 1 < width:
            scaled = row * (1.0 / pivot)
            left = width - 1 - j
            rest = work[(j + 1) * batch :, :].reshape(left, batch, 2 * width)
            rest = rest - rest[:, :, j : j + 1] * scaled[None]
            work[(j + 1) * batch :, :] = rest.reshape(left * batch, 2 * width)
        work[j * batch : (j + 1) * batch, :] = jnp.where(lane >= j, row * lax.rsqrt(pivot), 0.0)


def request_kernel(dest_ref, leaf_ref, tags_ref, place_ref):
    count = dest_ref.shape[1]
    across = jnp.broadcast_to(dest_ref[...].astype(f32), (count, count))
    down = across.T
    first, second = sublanes((count, count)), lanes((count, count))
    earlier = jnp.where((across == down) & (first < second), 1.0, 0.0)
    place = jnp.sum(earlier, axis=0, keepdims=True)
    named = across == first.astype(f32)
    leaf = jnp.broadcast_to(leaf_ref[...].astype(f32), (count, count))
    slot = jnp.broadcast_to(place, (count, count))
    tag_a = jnp.sum(jnp.where(named & (slot == 0.0), leaf, 0.0), axis=1, keepdims=True)
    tag_b = jnp.sum(jnp.where(named & (slot == 1.0), leaf, 0.0), axis=1, keepdims=True)
    tags = jnp.where(second == 0, tag_a, jnp.where(second == 1, tag_b, 0.0))
    tags_ref[...] = tags.astype(jnp.int32)
    place_ref[...] = place.astype(jnp.int32)


def requests(dests, col_leaf):
    count = dests.shape[1]
    return pl.pallas_call(
        request_kernel,
        out_shape=(
            jax.ShapeDtypeStruct((count, count), jnp.int32),
            jax.ShapeDtypeStruct((1, count), jnp.int32),
        ),
        cost_estimate=cost(1e5, 1e5),
        name="requests",
    )(dests, col_leaf)


def factor_kernel(leaves, width, basis_ref, rl_ref, triple_ref, pack_ref, pack_up_ref, work):
    step = pl.program_id(0)
    points = basis_ref.shape[2]
    x = basis_ref[...].reshape(2 * width, points)
    high, low = halves(x)
    both = jnp.concatenate([high, low], axis=0).astype(bf16)
    prod = lax.dot_general(both, both, (((1,), (1,)), ((), ())), preferred_element_type=f32)
    two = 2 * width
    gram = prod[:two, :two] + (prod[:two, two:] + prod[two:, :two]) + prod[two:, two:]
    work[pl.ds(2 * step, width, stride=leaves), :] = with_identity(gram[:width])
    work[pl.ds(2 * step + 1, width, stride=leaves), :] = with_identity(
        pltpu.roll(gram[width:], width, 1)
    )

    @pl.when(step == pl.num_programs(0) - 1)
    def _():
        eliminate(work, width, leaves)
        lane = lanes((two, two))
        half = width // 2
        target = lanes((two, width))
        source = jnp.where(target < half, 2 * target, 2 * (target - half) + 1)
        reorder = (sublanes((two, width)) == source).astype(f32).astype(bf16)
        for b in range(leaves):
            whole = work[pl.ds(b, width, stride=leaves), :]
            rl_ref[b] = whole
            even = work[pl.ds(b, half, stride=2 * leaves), :]
            odd = work[pl.ds(b + leaves, half, stride=2 * leaves), :]
            high, low = halves(jnp.concatenate([even, odd], axis=0))
            both = jnp.concatenate([high, low], axis=0).astype(bf16)
            moved = jnp.dot(both, reorder, preferred_element_type=f32)
            triple_ref[b] = jnp.concatenate(
                [moved[:width], moved[:width], moved[width:]], axis=1
            ).astype(bf16)
            padded = jnp.concatenate([whole, jnp.zeros_like(whole)], axis=0)
            lower = jnp.where(lane < width, padded, 0.0).T[:width]
            pack = jnp.concatenate(
                [
                    lower[48:64],
                    lower[32:48] + pltpu.roll(lower[0:16], 48, 1),
                    lower[16:24] + pltpu.roll(lower[24:32], 32, 1),
                ],
                axis=0,
            )
            pack_ref[b] = pack
            pack_up_ref[b] = pltpu.roll(pack, width, 1)


def leaf_factors(basis):
    leaves, width, points = basis.shape
    whole = lambda *shape: pl.BlockSpec(shape, lambda i: (0,) * len(shape))
    return pl.pallas_call(
        functools.partial(factor_kernel, leaves, width),
        grid=(leaves // 2,),
        in_specs=[pl.BlockSpec((2, width, points), lambda i: (i, 0, 0))],
        out_specs=[
            whole(leaves, width, 2 * width),
            whole(leaves, width, 3 * width),
            whole(leaves, ROWS, 2 * width),
            whole(leaves, ROWS, 2 * width),
        ],
        out_shape=[
            jax.ShapeDtypeStruct((leaves, width, 2 * width), f32),
            jax.ShapeDtypeStruct((leaves, width, 3 * width), bf16),
            jax.ShapeDtypeStruct((leaves, ROWS, 2 * width), f32),
            jax.ShapeDtypeStruct((leaves, ROWS, 2 * width), f32),
        ],
        scratch_shapes=[pltpu.VMEM((width * leaves, 2 * width), f32)],
        cost_estimate=cost(5e9, 6e6),
        name="leaf_factors",
    )(basis)


def reply_kernel(tags_ref, pack_ref, pack_up_ref, out_ref):
    step = pl.program_id(0)
    for r in range(out_ref.shape[0]):
        at = step * out_ref.shape[0] + r
        out_ref[r] = pack_ref[tags_ref[at, 0]] + pack_up_ref[tags_ref[at, 1]]


def replies(tags, pack, pack_up):
    peers = tags.shape[0]
    leaves, rows, wide = pack.shape
    table = pl.BlockSpec((leaves, rows, wide), lambda i: (0, 0, 0))
    return pl.pallas_call(
        reply_kernel,
        grid=(peers // 16,),
        in_specs=[pl.BlockSpec(memory_space=pltpu.SMEM), table, table],
        out_specs=pl.BlockSpec((16, rows, wide), lambda i: (i, 0, 0)),
        out_shape=jax.ShapeDtypeStruct((peers, rows, wide), f32),
        cost_estimate=cost(1e6, 4e6),
        name="replies",
    )(tags, pack, pack_up)


def split_rows(pair):
    width = pair.shape[1] // 2
    return jnp.concatenate([pair[:, :width], pair[:, width:]], axis=0)


def join_rows(square):
    half = square.shape[0] // 2
    return jnp.concatenate([square[:half], square[half:]], axis=1)


def pair_of(ref, n):
    return ref[pl.ds(n // 8 * 256 + n % 8, 32, stride=8), :]


def natural(pair, scratch):
    half, wide = pair.shape
    scratch[pl.ds(0, half, stride=2), :] = pair
    scratch[pl.ds(1, half, stride=2), :] = pltpu.roll(pair, wide // 2, 1)
    return scratch[:, : wide // 2]


def levels_kernel(triple_ref, leaf_ref, upper_ref, lifted_ref, one_ref, two_ref, scratch):
    leaves = triple_ref.shape[0]
    kept = None
    for c in range(leaves // 2):
        upper = natural(pair_of(upper_ref, c), scratch.at[c])
        lifted = []
        for n in (2 * c, 2 * c + 1):
            here = jnp.dot(
                triple_ref[n],
                right_triple(split_rows(pair_of(leaf_ref, n))),
                preferred_element_type=f32,
            )
            lifted_ref[n] = here
            lifted.append(here)
        stack = jnp.concatenate(lifted, axis=0)
        one_ref[c] = product(stack.T, stack)
        image = product(stack, upper)
        second = product(image.T, image)
        if c % 2:
            two_ref[c // 2] = jnp.concatenate([kept, second], axis=1)
        kept = second


def levels(triple, leaf_pairs, upper_pairs):
    leaves, width, _ = triple.shape
    return pl.pallas_call(
        levels_kernel,
        out_shape=[
            jax.ShapeDtypeStruct((leaves, width, width), f32),
            jax.ShapeDtypeStruct((leaves // 2, width, width), f32),
            jax.ShapeDtypeStruct((leaves // 4, width, 2 * width), f32),
        ],
        scratch_shapes=[pltpu.VMEM((leaves // 2, width, 2 * width), f32)],
        cost_estimate=cost(5e9, 2e6),
        name="levels",
    )(triple, leaf_pairs, upper_pairs)


def upper_kernel(one_ref, own_ref, other_ref, lifted_ref, upper_ref, leaf_out, upper_out, work, scratch):
    count, width, _ = one_ref.shape
    batch = 2 * count
    half = width // 2
    for c in range(count):
        one = one_ref[c]
        work[pl.ds(c, width, stride=batch), :] = with_identity(jnp.concatenate([one, one], axis=1))
        summed = own_ref[c // 2] + other_ref[c // 2]
        if c % 2:
            summed = pltpu.roll(summed, width, 1)
        work[pl.ds(count + c, width, stride=batch), :] = with_identity(summed)
    eliminate(work, width, batch)
    for c in range(count):
        inverse = work[pl.ds(c, width, stride=batch), :][:, width:].T
        for n in (2 * c, 2 * c + 1):
            new = product(lifted_ref[n], inverse)
            leaf_out[pl.ds(n // 8 * 256 + n % 8, half, stride=8), :] = join_rows(new)
        even = work[pl.ds(c, half, stride=2 * batch), :][:, :width]
        odd = work[pl.ds(c + batch, half, stride=2 * batch), :][:, :width]
        raised = product(
            jnp.concatenate([even, odd], axis=0), natural(pair_of(upper_ref, c), scratch.at[c])
        )
        inverse = work[pl.ds(count + c, width, stride=batch), :][:, width:].T
        new = product(raised, inverse)
        upper_out[pl.ds(c // 8 * 256 + c % 8, half, stride=8), :] = join_rows(new)


def uppers(one, own, other, lifted, upper_pairs):
    count, width, _ = one.shape
    return pl.pallas_call(
        upper_kernel,
        out_shape=[
            jax.ShapeDtypeStruct((2 * count * width // 2, 2 * width), f32),
            jax.ShapeDtypeStruct((count * width // 2, 2 * width), f32),
        ],
        scratch_shapes=[
            pltpu.VMEM((width * 2 * count, 2 * width), f32),
            pltpu.VMEM((count, width, 2 * width), f32),
        ],
        cost_estimate=cost(5e9, 2e6),
        name="uppers",
    )(one, own, other, lifted, upper_pairs)


def ortho_kernel(factor, rl_ref, basis_ref, out_ref):
    width = basis_ref.shape[1]
    for n in range(basis_ref.shape[0]):
        out_ref[n] = product(rl_ref[n][:, width:] * factor, basis_ref[n])


def ortho(rl, basis):
    leaves, width, points = basis.shape
    return pl.pallas_call(
        functools.partial(ortho_kernel, math.sqrt(points)),
        grid=(leaves // 2,),
        in_specs=[
            pl.BlockSpec((2, width, 2 * width), lambda i: (i, 0, 0)),
            pl.BlockSpec((2, width, points), lambda i: (i, 0, 0)),
        ],
        out_specs=pl.BlockSpec((2, width, points), lambda i: (i, 0, 0)),
        out_shape=jax.ShapeDtypeStruct(basis.shape, f32),
        cost_estimate=cost(5e9, 8e6),
        name="ortho",
    )(rl, basis)


def left_kernel(row_ref, triple_ref, coupling_ref, out_ref):
    step = pl.program_id(0)
    for i in range(8):
        block = split_rows(coupling_ref[pl.ds(i, 32, stride=8), :])
        left = jnp.dot(
            triple_ref[row_ref[0, step * 8 + i]], right_triple(block), preferred_element_type=f32
        )
        out_ref[i] = left_triple(left)


def lefts(row_leaf, triple, coupling_pairs):
    blocks = row_leaf.shape[1]
    leaves, width, _ = triple.shape
    return pl.pallas_call(
        left_kernel,
        grid=(blocks // 8,),
        in_specs=[
            pl.BlockSpec(memory_space=pltpu.SMEM),
            pl.BlockSpec(triple.shape, lambda i: (0, 0, 0)),
            pl.BlockSpec((8 * width // 2, 2 * width), lambda i: (i, 0)),
        ],
        out_specs=pl.BlockSpec((8, width, 3 * width), lambda i: (i, 0, 0)),
        out_shape=jax.ShapeDtypeStruct((blocks, width, 3 * width), bf16),
        cost_estimate=cost(5e9, 6e6),
        name="lefts",
    )(row_leaf, triple, coupling_pairs)


def unpack(pack, place):
    shift = place * 64
    lane = lanes((16, 128))
    first = pltpu.roll(pack[0:16], shift, 1)
    middle = pltpu.roll(pack[16:32], shift, 1)
    corner = pltpu.roll(pack[16:32], lax.rem(shift + 80, 128), 1)
    upper = pltpu.roll(pack[32:40], shift, 1)
    lower = pltpu.roll(pack[32:40], lax.rem(shift + 96, 128), 1)
    narrow = lane[:8] < 32
    return jnp.concatenate(
        [
            jnp.where(lane < 16, corner, 0.0),
            jnp.where(narrow, upper, 0.0),
            jnp.where(narrow, lower, 0.0),
            jnp.where(lane < 48, middle, 0.0),
            first,
        ],
        axis=0,
    )


def finish_kernel(dest_ref, place_ref, left_ref, pack_ref, out_ref):
    step = pl.program_id(0)
    width = left_ref.shape[1]
    for i in range(8):
        at = step * 8 + i
        column = unpack(pack_ref[dest_ref[0, at]], place_ref[0, at])[:, :width]
        done = jnp.dot(left_ref[i], right_triple(column), preferred_element_type=f32)
        out_ref[pl.ds(i, width // 2, stride=8), :] = join_rows(done)


def finish(dests, place, left, packs):
    blocks, width, wide = left.shape
    scalar = pl.BlockSpec(memory_space=pltpu.SMEM)
    return pl.pallas_call(
        finish_kernel,
        grid=(blocks // 8,),
        in_specs=[
            scalar,
            scalar,
            pl.BlockSpec((8, width, wide), lambda i: (i, 0, 0)),
            pl.BlockSpec(packs.shape, lambda i: (0, 0, 0), pipeline_mode=pl.Buffered(1)),
        ],
        out_specs=pl.BlockSpec((8 * width // 2, 2 * width), lambda i: (i, 0)),
        out_shape=jax.ShapeDtypeStruct((blocks * width // 2, 2 * width), f32),
        cost_estimate=cost(5e9, 8e6),
        name="finish",
    )(dests, place, left, packs)


def to_pairs(rows):
    count, square = rows.shape
    tiles = rows.reshape(count // 8, 8, square // 128, 128).transpose(0, 2, 1, 3)
    return tiles.reshape(count * square // 128, 128)


def from_pairs(pairs, square):
    count = pairs.shape[0] * 128 // square
    tiles = pairs.reshape(count // 8, square // 128, 8, 128).transpose(0, 2, 1, 3)
    return tiles.reshape(count, square)


def shards(basis, leaf_transfer, upper_transfer, coupling, row_leaf, col_dev, col_leaf):
    blocks, square = coupling.shape
    dests = col_dev.reshape(1, blocks)
    tags, place = requests(dests, col_leaf.reshape(1, blocks))
    asked = lax.all_to_all(tags, BOTH, split_axis=0, concat_axis=0, tiled=True)
    rl, triple, pack, pack_up = leaf_factors(basis)
    packs = lax.all_to_all(
        replies(asked, pack, pack_up), BOTH, split_axis=0, concat_axis=0, tiled=True
    )
    upper_pairs = to_pairs(upper_transfer)
    lifted, one, own = levels(triple, to_pairs(leaf_transfer), upper_pairs)
    size = lax.axis_size("grp")
    other = lax.ppermute(own, "grp", [(i, i ^ 1) for i in range(size)])
    left = lefts(row_leaf.reshape(1, blocks), triple, to_pairs(coupling))
    ortho_basis = ortho(rl, basis)
    leaf_out, upper_out = uppers(one, own, other, lifted, upper_pairs)
    coupling_out = finish(dests, place, left, packs)
    return (
        ortho_basis,
        from_pairs(leaf_out, square),
        from_pairs(upper_out, square),
        from_pairs(coupling_out, square),
    )


def solution(mesh):
    both = P(BOTH, None)
    in_specs = (P(BOTH, None, None), both, both, both, P(BOTH), both, P(BOTH))
    out_specs = (P(BOTH, None, None), both, both, both)
    return jax.shard_map(shards, mesh=mesh, in_specs=in_specs, out_specs=out_specs, check_vma=False)
```

```python
import functools
import math

import jax
import jax.numpy as jnp
from jax import lax
from jax.experimental import pallas as pl
from jax.experimental.pallas import tpu as pltpu
from jax.sharding import PartitionSpec as P

BOTH = ("grp", "dev")
ROWS = 36
ROOM = pltpu.CompilerParams(vmem_limit_bytes=24 << 20)
VMEM = pl.BlockSpec(memory_space=pltpu.VMEM)
HBM = pl.BlockSpec(memory_space=pltpu.HBM)
bf16, f32 = jnp.bfloat16, jnp.float32


def cost(flops, moved):
    return pl.CostEstimate(flops=int(flops), bytes_accessed=int(moved), transcendentals=0)


def halves(x):
    high = x.astype(bf16).astype(f32)
    return high, x - high


def left_triple(x):
    high, low = halves(x)
    return jnp.concatenate([high, high, low], axis=1).astype(bf16)


def right_triple(x):
    high, low = halves(x)
    return jnp.concatenate([high, low, high], axis=0).astype(bf16)


def product(first, second):
    return jnp.dot(left_triple(first), right_triple(second), preferred_element_type=f32)


def lanes(shape):
    return lax.broadcasted_iota(jnp.int32, shape, len(shape) - 1)


def sublanes(shape):
    return lax.broadcasted_iota(jnp.int32, shape, len(shape) - 2)


def with_identity(square):
    lane, row = lanes(square.shape), sublanes(square.shape)
    return jnp.where(lane < square.shape[0], square, (lane == row + square.shape[0]).astype(f32))


def eliminate(work, width, batch):
    wide = 2 * width
    lane = lanes((batch, wide))

    def store(i, value):
        work[i * batch : (i + 1) * batch, :] = jnp.where(lane >= i, value, 0.0)

    for j in range(0, width, 4):
        r0, r1, r2, r3 = [work[(j + k) * batch : (j + k + 1) * batch, :] for k in range(4)]
        at = lambda row, k: jnp.broadcast_to(row[:, j + k : j + k + 1], (batch, wide))
        a, b, c = at(r0, 0), at(r0, 1), at(r1, 1)
        p02, p03, p12, p13 = at(r0, 2), at(r0, 3), at(r1, 2), at(r1, 3)
        det = a * c - b * b
        inv = 1.0 / det
        x00, x10 = (c * p02 - b * p12) * inv, (a * p12 - b * p02) * inv
        x01, x11 = (c * p03 - b * p13) * inv, (a * p13 - b * p03) * inv
        s00 = at(r2, 2) - (p02 * x00 + p12 * x10)
        s01 = at(r2, 3) - (p02 * x01 + p12 * x11)
        s11 = at(r3, 3) - (p03 * x01 + p13 * x11)
        det_s = s00 * s11 - s01 * s01
        inv_s = 1.0 / det_s
        q2 = r2 - x00 * r0 - x10 * r1
        q3 = r3 - x01 * r0 - x11 * r1
        n1 = a * r1 - b * r0
        n3 = s00 * q3 - s01 * q2
        left = width - 4 - j
        if left:
            w0, w1 = (s11 * q2 - s01 * q3) * inv_s, n3 * inv_s
            v0 = (c * r0 - b * r1) * inv - x00 * w0 - x01 * w1
            v1 = n1 * inv - x10 * w0 - x11 * w1
            rest = work[(j + 4) * batch :, :].reshape(left, batch, wide)
            col = lambda k: rest[:, :, j + k : j + k + 1]
            rest = rest - ((col(0) * v0 + col(1) * v1) + (col(2) * w0 + col(3) * w1))
            work[(j + 4) * batch :, :] = rest.reshape(left * batch, wide)
        ra, rs = lax.rsqrt(a), lax.rsqrt(s00)
        store(j, r0 * ra)
        store(j + 1, n1 * (ra * lax.rsqrt(det)))
        store(j + 2, q2 * rs)
        store(j + 3, n3 * (rs * lax.rsqrt(det_s)))


def eliminate_small(work, width, batch):
    wide = 2 * width
    lane = lanes((batch, wide))
    rows = [work[i * batch : (i + 1) * batch, :] for i in range(width)]
    at = lambda row, k: jnp.broadcast_to(row[:, k : k + 1], (batch, wide))

    def store(i, value):
        work[i * batch : (i + 1) * batch, :] = jnp.where(lane >= i, value, 0.0)

    for j in range(0, width, 2):
        r0, r1 = rows[j], rows[j + 1]
        a, b, c = at(r0, j), at(r0, j + 1), at(r1, j + 1)
        det = a * c - b * b
        inv = 1.0 / det
        n0, n1 = c * r0 - b * r1, a * r1 - b * r0
        for i in range(j + 2, width):
            rows[i] = rows[i] - (at(rows[i], j) * n0 + at(rows[i], j + 1) * n1) * inv
        ra = lax.rsqrt(a)
        store(j, r0 * ra)
        store(j + 1, n1 * (ra * lax.rsqrt(det)))


def request_kernel(dest_ref, leaf_ref, tags_ref, place_ref):
    count = dest_ref.shape[1]
    across = jnp.broadcast_to(dest_ref[...].astype(f32), (count, count))
    down = across.T
    first, second = sublanes((count, count)), lanes((count, count))
    earlier = jnp.where((across == down) & (first < second), 1.0, 0.0)
    place = jnp.sum(earlier, axis=0, keepdims=True)
    named = across == first.astype(f32)
    leaf = jnp.broadcast_to(leaf_ref[...].astype(f32), (count, count))
    slot = jnp.broadcast_to(place, (count, count))
    tag_a = jnp.sum(jnp.where(named & (slot == 0.0), leaf, 0.0), axis=1, keepdims=True)
    tag_b = jnp.sum(jnp.where(named & (slot == 1.0), leaf, 0.0), axis=1, keepdims=True)
    tags = jnp.where(second == 0, tag_a, jnp.where(second == 1, tag_b, 0.0))
    tags_ref[...] = tags.astype(jnp.int32)
    place_ref[...] = place.astype(jnp.int32)


def requests(dests, col_leaf):
    count = dests.shape[1]
    return pl.pallas_call(
        request_kernel,
        out_shape=(
            jax.ShapeDtypeStruct((count, count), jnp.int32),
            jax.ShapeDtypeStruct((1, count), jnp.int32),
        ),
        cost_estimate=cost(1e5, 1e5),
        name="requests",
    )(dests, col_leaf)


def pack_rows(lower):
    moved = lambda start, stop, lane: pltpu.roll(lower[start:stop], lane, 1)
    quarter = lower[24:32]
    last = quarter + pltpu.roll(pltpu.roll(quarter, 4, 0), 32, 1)
    return jnp.concatenate(
        [
            lower[56:64],
            lower[48:56] + moved(0, 8, 56),
            lower[40:48] + moved(8, 16, 48),
            lower[32:40] + moved(16, 24, 40),
            jnp.where(sublanes(last.shape) < 4, last, 0.0),
        ],
        axis=0,
    )


def factor_kernel(
    leaves, width, source_ref, rl_ref, triple_ref, pack_ref, pack_up_ref, work, basis_ref, sems
):
    count, _, points = basis_ref.shape
    pieces = sems.shape[0]
    size = count // pieces
    copies = [
        pltpu.make_async_copy(
            source_ref.at[pl.ds(p * size, size)], basis_ref.at[pl.ds(p * size, size)], sems.at[p]
        )
        for p in range(pieces)
    ]
    for copy in copies:
        copy.start()
    two = 2 * width
    for q in range(0, count, 2):
        if q % size == 0:
            copies[q // size].wait()
        high, low = halves(basis_ref[q : q + 2].reshape(two, points))
        both = jnp.concatenate([high, low], axis=0).astype(bf16)
        prod = lax.dot_general(both, both, (((1,), (1,)), ((), ())), preferred_element_type=f32)
        gram = prod[:two, :two] + (prod[:two, two:] + prod[two:, :two]) + prod[two:, two:]
        work[pl.ds(q, width, stride=leaves), :] = with_identity(gram[:width])
        work[pl.ds(q + 1, width, stride=leaves), :] = with_identity(
            pltpu.roll(gram[width:], width, 1)
        )

    eliminate(work, width, leaves)
    lane = lanes((two, two))
    half = width // 2
    target = lanes((two, width))
    source = jnp.where(target < half, 2 * target, 2 * (target - half) + 1)
    reorder = (sublanes((two, width)) == source).astype(f32).astype(bf16)
    for b in range(leaves):
        whole = work[pl.ds(b, width, stride=leaves), :]
        rl_ref[b] = whole
        even = work[pl.ds(b, half, stride=2 * leaves), :]
        odd = work[pl.ds(b + leaves, half, stride=2 * leaves), :]
        high, low = halves(jnp.concatenate([even, odd], axis=0))
        both = jnp.concatenate([high, low], axis=0).astype(bf16)
        moved = jnp.dot(both, reorder, preferred_element_type=f32)
        triple_ref[b] = jnp.concatenate(
            [moved[:width], moved[:width], moved[width:]], axis=1
        ).astype(bf16)
        padded = jnp.concatenate([whole, jnp.zeros_like(whole)], axis=0)
        lower = jnp.where(lane < width, padded, 0.0).T[:width]
        pack = pack_rows(lower)
        pack_ref[b] = pack
        pack_up_ref[b] = pltpu.roll(pack, width, 1)


def leaf_factors(basis):
    leaves, width, points = basis.shape
    return pl.pallas_call(
        functools.partial(factor_kernel, leaves, width),
        in_specs=[HBM],
        out_specs=[VMEM] * 4,
        out_shape=[
            jax.ShapeDtypeStruct((leaves, width, 2 * width), f32),
            jax.ShapeDtypeStruct((leaves, width, 3 * width), bf16),
            jax.ShapeDtypeStruct((leaves, 40, 2 * width), f32),
            jax.ShapeDtypeStruct((leaves, 40, 2 * width), f32),
        ],
        scratch_shapes=[
            pltpu.VMEM((width * leaves, 2 * width), f32),
            pltpu.VMEM(basis.shape, f32),
            pltpu.SemaphoreType.DMA((leaves // 4,)),
        ],
        compiler_params=pltpu.CompilerParams(vmem_limit_bytes=53248 << 10),
        cost_estimate=cost(5e9, 6e6),
        name="leaf_factors",
    )(basis)


def reply_kernel(tags_ref, pack_ref, pack_up_ref, out_ref, line, table, sem):
    step = pl.program_id(0)
    count = out_ref.shape[0] // ROWS

    @pl.when(step == 0)
    def _():
        line[...] = tags_ref[...].astype(f32).T[:8].astype(jnp.int32)
        copy = pltpu.make_async_copy(line, table, sem)
        copy.start()
        copy.wait()

    for r in range(0, count, 2):
        at = step * count + r
        even = pack_ref[table[0, at]] + pack_up_ref[table[1, at]]
        odd = pack_ref[table[0, at + 1]] + pack_up_ref[table[1, at + 1]]
        odd = pltpu.roll(odd, 4, 0)
        out_ref[r * ROWS : r * ROWS + 32] = even[:32]
        out_ref[r * ROWS + 32 : r * ROWS + 40] = even[32:] + odd[:8]
        out_ref[r * ROWS + 40 : (r + 2) * ROWS] = odd[8:]


def replies(tags, pack, pack_up):
    peers = tags.shape[0]
    leaves, rows, wide = pack.shape
    table = pl.BlockSpec((leaves, rows, wide), lambda i: (0, 0, 0))
    per = peers // 2
    return pl.pallas_call(
        reply_kernel,
        grid=(peers // per,),
        in_specs=[pl.BlockSpec(tags.shape, lambda i: (0, 0)), table, table],
        out_specs=pl.BlockSpec((per * ROWS, wide), lambda i: (i, 0)),
        out_shape=jax.ShapeDtypeStruct((peers * ROWS, wide), f32),
        scratch_shapes=[
            pltpu.VMEM((8, peers), jnp.int32),
            pltpu.SMEM((8, peers), jnp.int32),
            pltpu.SemaphoreType.DMA,
        ],
        compiler_params=ROOM,
        cost_estimate=cost(1e6, 4e6),
        name="replies",
    )(tags, pack, pack_up)


def split_rows(pair):
    width = pair.shape[1] // 2
    return jnp.concatenate([pair[:, :width], pair[:, width:]], axis=0)


def join_rows(square):
    half = square.shape[0] // 2
    return jnp.concatenate([square[:half], square[half:]], axis=1)


def pair_of(ref, n):
    return ref[pl.ds(n // 8 * 256 + n % 8, 32, stride=8), :]


def natural(pair, scratch):
    half, wide = pair.shape
    scratch[pl.ds(0, half, stride=2), :] = pair
    scratch[pl.ds(1, half, stride=2), :] = pltpu.roll(pair, wide // 2, 1)
    return scratch[:, : wide // 2]


def levels_kernel(triple_ref, leaf_ref, upper_ref, lifted_ref, one_ref, two_ref, scratch):
    leaves = triple_ref.shape[0]
    kept = None
    for c in range(leaves // 2):
        upper = natural(pair_of(upper_ref, c), scratch.at[c])
        lifted = []
        for n in (2 * c, 2 * c + 1):
            here = jnp.dot(
                triple_ref[n],
                right_triple(split_rows(pair_of(leaf_ref, n))),
                preferred_element_type=f32,
            )
            lifted_ref[n] = here
            lifted.append(here)
        stack = jnp.concatenate(lifted, axis=0)
        one_ref[c] = product(stack.T, stack)
        image = product(stack, upper)
        second = product(image.T, image)
        if c % 2:
            two_ref[c // 2] = jnp.concatenate([kept, second], axis=1)
        kept = second


def levels(triple, leaf_pairs, upper_pairs):
    leaves, width, _ = triple.shape
    return pl.pallas_call(
        levels_kernel,
        out_shape=[
            jax.ShapeDtypeStruct((leaves, width, width), f32),
            jax.ShapeDtypeStruct((leaves // 2, width, width), f32),
            jax.ShapeDtypeStruct((leaves // 4, width, 2 * width), f32),
        ],
        scratch_shapes=[pltpu.VMEM((leaves // 2, width, 2 * width), f32)],
        compiler_params=ROOM,
        cost_estimate=cost(5e9, 2e6),
        name="levels",
    )(triple, leaf_pairs, upper_pairs)


def one_kernel(one_ref, lifted_ref, upper_ref, leaf_out, raised_out, work, scratch):
    count, width, _ = one_ref.shape
    half = width // 2
    for c in range(count):
        one = one_ref[c]
        work[pl.ds(c, width, stride=count), :] = with_identity(jnp.concatenate([one, one], axis=1))
    eliminate_small(work, width, count)
    for c in range(count):
        inverse = work[pl.ds(c, width, stride=count), :][:, width:].T
        for n in (2 * c, 2 * c + 1):
            new = product(lifted_ref[n], inverse)
            leaf_out[pl.ds(n // 8 * 256 + n % 8, half, stride=8), :] = join_rows(new)
        even = work[pl.ds(c, half, stride=2 * count), :][:, :width]
        odd = work[pl.ds(c + count, half, stride=2 * count), :][:, :width]
        raised_out[c] = product(
            jnp.concatenate([even, odd], axis=0), natural(pair_of(upper_ref, c), scratch.at[c])
        )


def level_one(one, lifted, upper_pairs):
    count, width, _ = one.shape
    return pl.pallas_call(
        one_kernel,
        in_specs=[VMEM] * 3,
        out_specs=[VMEM] * 2,
        out_shape=[
            jax.ShapeDtypeStruct((count * width, 2 * width), f32),
            jax.ShapeDtypeStruct((count, width, width), f32),
        ],
        scratch_shapes=[
            pltpu.VMEM((width * count, 2 * width), f32),
            pltpu.VMEM((count, width, 2 * width), f32),
        ],
        compiler_params=ROOM,
        cost_estimate=cost(3e9, 2e6),
        name="level_one",
    )(one, lifted, upper_pairs)


def two_kernel(own_ref, other_ref, raised_ref, upper_out, work):
    count, width, _ = raised_ref.shape
    for c in range(count):
        summed = own_ref[c // 2] + other_ref[c // 2]
        if c % 2:
            summed = pltpu.roll(summed, width, 1)
        work[pl.ds(c, width, stride=count), :] = with_identity(summed)
    eliminate_small(work, width, count)
    for c in range(count):
        inverse = work[pl.ds(c, width, stride=count), :][:, width:].T
        new = product(raised_ref[c], inverse)
        upper_out[pl.ds(c // 8 * 256 + c % 8, width // 2, stride=8), :] = join_rows(new)


def level_two(own, other, raised):
    count, width, _ = raised.shape
    return pl.pallas_call(
        two_kernel,
        in_specs=[VMEM] * 3,
        out_specs=VMEM,
        out_shape=jax.ShapeDtypeStruct((count * width // 2, 2 * width), f32),
        scratch_shapes=[pltpu.VMEM((width * count, 2 * width), f32)],
        compiler_params=ROOM,
        cost_estimate=cost(1e9, 1e6),
        name="level_two",
    )(own, other, raised)


def ortho_kernel(factor, rl_ref, basis_ref, out_ref):
    width = basis_ref.shape[1]
    for n in range(basis_ref.shape[0]):
        out_ref[n] = product(rl_ref[n][:, width:] * factor, basis_ref[n])


def ortho(rl, basis):
    leaves, width, points = basis.shape
    return pl.pallas_call(
        functools.partial(ortho_kernel, math.sqrt(points)),
        grid=(2,),
        in_specs=[
            pl.BlockSpec((leaves // 2, width, 2 * width), lambda i: (i, 0, 0)),
            pl.BlockSpec((leaves // 2, width, points), lambda i: (i, 0, 0)),
        ],
        out_specs=pl.BlockSpec((leaves // 2, width, points), lambda i: (i, 0, 0)),
        out_shape=jax.ShapeDtypeStruct(basis.shape, f32),
        compiler_params=ROOM,
        cost_estimate=cost(5e9, 8e6),
        name="ortho",
    )(rl, basis)


def left_kernel(row_ref, triple_ref, coupling_ref, out_ref):
    step = pl.program_id(0)
    count = 2 * out_ref.shape[0]

    def group(g, _):
        for q in range(16):
            at = g * 32 + 2 * q
            pair = []
            for i in range(2):
                block = coupling_ref[pl.ds(g * 1024 + q // 4 * 256 + (2 * q + i) % 8, 32, stride=8), :]
                pair.append(
                    jnp.dot(
                        triple_ref[row_ref[0, step * count + at + i]],
                        right_triple(split_rows(block)),
                        preferred_element_type=f32,
                    )
                )
            high, low = halves(jnp.concatenate(pair, axis=1))
            out_ref[g * 16 + q] = jnp.concatenate([high, low], axis=0).astype(bf16)
        return 0

    lax.fori_loop(0, count // 32, group, 0)


def lefts(row_leaf, triple, coupling_pairs):
    blocks = row_leaf.shape[1]
    leaves, width, _ = triple.shape
    wide = 2 * width
    per = blocks // 2
    return pl.pallas_call(
        left_kernel,
        grid=(blocks // per,),
        in_specs=[
            pl.BlockSpec(memory_space=pltpu.SMEM),
            pl.BlockSpec(triple.shape, lambda i: (0, 0, 0)),
            pl.BlockSpec((per * width // 2, wide), lambda i: (i, 0)),
        ],
        out_specs=pl.BlockSpec((per // 2, wide, wide), lambda i: (i, 0, 0)),
        out_shape=jax.ShapeDtypeStruct((blocks // 2, wide, wide), bf16),
        compiler_params=ROOM,
        cost_estimate=cost(5e9, 6e6),
        name="lefts",
    )(row_leaf, triple, coupling_pairs)


def unpack(ref, base, place, side):
    lane = lanes((8, 128)) - 64 * side
    shift = (place ^ side) * 64

    def piece(rows, start, count):
        turned = pltpu.roll(rows, lax.rem(shift + (128 - start), 128), 1)
        return jnp.where((lane >= 0) & (lane < count), turned, 0.0)

    first, second, third, fourth = [ref[pl.ds(base + 8 * k, 8), :] for k in range(4)]
    last = ref[pl.ds(base + 28, 8), :]
    middle = jnp.where(
        sublanes((8, 128)) < 4,
        pltpu.roll(piece(last, 0, 32), 4, 0),
        piece(last, 32, 32),
    )
    return jnp.concatenate(
        [
            piece(second, 56, 8),
            piece(third, 48, 16),
            piece(fourth, 40, 24),
            middle,
            piece(fourth, 0, 40),
            piece(third, 0, 48),
            piece(second, 0, 56),
            piece(first, 0, 64),
        ],
        axis=0,
    )


def finish_kernel(
    dest_ref, place_ref, left_hbm, pack_ref, out_hbm, left_ref, out_ref, in_sems, out_sems
):
    pairs, wide, _ = left_ref.shape
    width = wide // 2
    lane = lanes((width // 2, wide))
    groups = in_sems.shape[0]
    size = pairs // groups
    rows = size * wide // 2

    def fetch(g):
        part = pl.ds(g * size, size)
        return pltpu.make_async_copy(left_hbm.at[part], left_ref.at[part], in_sems.at[g])

    def put(g):
        part = pl.ds(pl.multiple_of(g * rows, rows), rows)
        return pltpu.make_async_copy(out_ref.at[part], out_hbm.at[part], out_sems.at[g])

    for g in range(groups):
        fetch(g).start()

    def group(g, _):
        fetch(g).wait()
        for q in range(size):
            lower = []
            for i in range(2):
                at = (g * size + q) * 2 + i
                lower.append(unpack(pack_ref, dest_ref[0, at] * ROWS, place_ref[0, at], i))
            high, low = halves(jnp.concatenate(lower, axis=0))
            left = left_ref[g * size + q]
            both = jnp.dot(left, high.astype(bf16), preferred_element_type=f32)
            done = (
                both[:width]
                + both[width:]
                + jnp.dot(left[:width], low.astype(bf16), preferred_element_type=f32)
            )
            even, odd = done[: width // 2], done[width // 2 :]
            base = g * rows + q // 4 * 256 + 2 * q % 8
            out_ref[pl.ds(base, 32, stride=8), :] = jnp.where(
                lane < width, even, pltpu.roll(odd, width, 1)
            )
            out_ref[pl.ds(base + 1, 32, stride=8), :] = jnp.where(
                lane < width, pltpu.roll(even, width, 1), odd
            )
        put(g).start()
        return 0

    lax.fori_loop(0, groups, group, 0)
    for g in range(groups):
        put(g).wait()


def finish(dests, place, left, packs):
    pairs, wide, _ = left.shape
    scalar = pl.BlockSpec(memory_space=pltpu.SMEM)
    shape = (pairs * wide // 2, wide)
    return pl.pallas_call(
        finish_kernel,
        in_specs=[scalar, scalar, HBM, VMEM],
        out_specs=HBM,
        out_shape=jax.ShapeDtypeStruct(shape, f32),
        scratch_shapes=[
            pltpu.VMEM(left.shape, bf16),
            pltpu.VMEM(shape, f32),
            pltpu.SemaphoreType.DMA((4,)),
            pltpu.SemaphoreType.DMA((4,)),
        ],
        compiler_params=pltpu.CompilerParams(vmem_limit_bytes=53248 << 10),
        cost_estimate=cost(5e9, 8e6),
        name="finish",
    )(dests, place, left, packs)


def to_pairs(rows):
    count, square = rows.shape
    tiles = rows.reshape(count // 8, 8, square // 128, 128).transpose(0, 2, 1, 3)
    return tiles.reshape(count * square // 128, 128)


def from_pairs(pairs, square):
    count = pairs.shape[0] * 128 // square
    tiles = pairs.reshape(count // 8, square // 128, 8, 128).transpose(0, 2, 1, 3)
    return tiles.reshape(count, square)


def shards(basis, leaf_transfer, upper_transfer, coupling, row_leaf, col_dev, col_leaf):
    blocks, square = coupling.shape
    dests = col_dev.reshape(1, blocks)
    tags, place = requests(dests, col_leaf.reshape(1, blocks))
    asked = lax.all_to_all(tags, BOTH, split_axis=0, concat_axis=0, tiled=True)
    rl, triple, pack, pack_up = leaf_factors(basis)
    answers = replies(asked, pack, pack_up).reshape(asked.shape[0], 1, -1)
    packs = lax.all_to_all(answers, BOTH, split_axis=0, concat_axis=0, tiled=True)
    packs = packs.reshape(-1, pack.shape[2])
    upper_pairs = to_pairs(upper_transfer)
    lifted, one, own = levels(triple, to_pairs(leaf_transfer), upper_pairs)
    size = lax.axis_size("grp")
    other = lax.ppermute(own, "grp", [(i, i ^ 1) for i in range(size)])
    left = lefts(row_leaf.reshape(1, blocks), triple, to_pairs(coupling))
    ortho_basis = ortho(rl, basis)
    leaf_out, raised = level_one(one, lifted, upper_pairs)
    upper_out = level_two(own, other, raised)
    coupling_out = finish(dests, place, left, packs)
    return (
        ortho_basis,
        from_pairs(leaf_out, square),
        from_pairs(upper_out, square),
        from_pairs(coupling_out, square),
    )


def solution(mesh):
    both = P(BOTH, None)
    in_specs = (P(BOTH, None, None), both, both, both, P(BOTH), both, P(BOTH))
    out_specs = (P(BOTH, None, None), both, both, both)
    return jax.shard_map(shards, mesh=mesh, in_specs=in_specs, out_specs=out_specs, check_vma=False)
```

```python
import functools
import math

import jax
import jax.numpy as jnp
from jax import lax
from jax.experimental import pallas as pl
from jax.experimental.pallas import tpu as pltpu
from jax.sharding import PartitionSpec as P

BOTH = ("grp", "dev")
ROWS = 34
ROOM = pltpu.CompilerParams(vmem_limit_bytes=24 << 20)
VMEM = pl.BlockSpec(memory_space=pltpu.VMEM)
HBM = pl.BlockSpec(memory_space=pltpu.HBM)
bf16, f32 = jnp.bfloat16, jnp.float32


def cost(flops, moved):
    return pl.CostEstimate(flops=int(flops), bytes_accessed=int(moved), transcendentals=0)


def halves(x):
    high = x.astype(bf16).astype(f32)
    return high, x - high


def left_triple(x):
    high, low = halves(x)
    return jnp.concatenate([high, high, low], axis=1).astype(bf16)


def right_triple(x):
    high, low = halves(x)
    return jnp.concatenate([high, low, high], axis=0).astype(bf16)


def product(first, second):
    return jnp.dot(left_triple(first), right_triple(second), preferred_element_type=f32)


def lanes(shape):
    return lax.broadcasted_iota(jnp.int32, shape, len(shape) - 1)


def sublanes(shape):
    return lax.broadcasted_iota(jnp.int32, shape, len(shape) - 2)


def with_identity(square):
    lane, row = lanes(square.shape), sublanes(square.shape)
    return jnp.where(lane < square.shape[0], square, (lane == row + square.shape[0]).astype(f32))


def eliminate(work, width, batch):
    wide = 2 * width
    lane = lanes((batch, wide))

    def store(i, value):
        work[i * batch : (i + 1) * batch, :] = jnp.where(lane >= i, value, 0.0)

    for j in range(0, width, 4):
        r0, r1, r2, r3 = [work[(j + k) * batch : (j + k + 1) * batch, :] for k in range(4)]
        at = lambda row, k: jnp.broadcast_to(row[:, j + k : j + k + 1], (batch, wide))
        a, b, c = at(r0, 0), at(r0, 1), at(r1, 1)
        p02, p03, p12, p13 = at(r0, 2), at(r0, 3), at(r1, 2), at(r1, 3)
        det = a * c - b * b
        inv = 1.0 / det
        x00, x10 = (c * p02 - b * p12) * inv, (a * p12 - b * p02) * inv
        x01, x11 = (c * p03 - b * p13) * inv, (a * p13 - b * p03) * inv
        s00 = at(r2, 2) - (p02 * x00 + p12 * x10)
        s01 = at(r2, 3) - (p02 * x01 + p12 * x11)
        s11 = at(r3, 3) - (p03 * x01 + p13 * x11)
        det_s = s00 * s11 - s01 * s01
        inv_s = 1.0 / det_s
        q2 = r2 - x00 * r0 - x10 * r1
        q3 = r3 - x01 * r0 - x11 * r1
        n1 = a * r1 - b * r0
        n3 = s00 * q3 - s01 * q2
        left = width - 4 - j
        if left:
            w0, w1 = (s11 * q2 - s01 * q3) * inv_s, n3 * inv_s
            v0 = (c * r0 - b * r1) * inv - x00 * w0 - x01 * w1
            v1 = n1 * inv - x10 * w0 - x11 * w1
            rest = work[(j + 4) * batch :, :].reshape(left, batch, wide)
            col = lambda k: rest[:, :, j + k : j + k + 1]
            rest = rest - ((col(0) * v0 + col(1) * v1) + (col(2) * w0 + col(3) * w1))
            work[(j + 4) * batch :, :] = rest.reshape(left * batch, wide)
        ra, rs = lax.rsqrt(a), lax.rsqrt(s00)
        store(j, r0 * ra)
        store(j + 1, n1 * (ra * lax.rsqrt(det)))
        store(j + 2, q2 * rs)
        store(j + 3, n3 * (rs * lax.rsqrt(det_s)))


def eliminate_small(work, width, batch):
    wide = 2 * width
    lane = lanes((batch, wide))
    rows = [work[i * batch : (i + 1) * batch, :] for i in range(width)]
    at = lambda row, k: jnp.broadcast_to(row[:, k : k + 1], (batch, wide))

    def store(i, value):
        work[i * batch : (i + 1) * batch, :] = jnp.where(lane >= i, value, 0.0)

    for j in range(0, width, 2):
        r0, r1 = rows[j], rows[j + 1]
        a, b, c = at(r0, j), at(r0, j + 1), at(r1, j + 1)
        det = a * c - b * b
        inv = 1.0 / det
        n0, n1 = c * r0 - b * r1, a * r1 - b * r0
        for i in range(j + 2, width):
            rows[i] = rows[i] - (at(rows[i], j) * n0 + at(rows[i], j + 1) * n1) * inv
        ra = lax.rsqrt(a)
        store(j, r0 * ra)
        store(j + 1, n1 * (ra * lax.rsqrt(det)))


def request_kernel(dest_ref, leaf_ref, tags_ref, place_ref):
    count = dest_ref.shape[1]
    across = jnp.broadcast_to(dest_ref[...].astype(f32), (count, count))
    down = across.T
    first, second = sublanes((count, count)), lanes((count, count))
    earlier = jnp.where((across == down) & (first < second), 1.0, 0.0)
    place = jnp.sum(earlier, axis=0, keepdims=True)
    named = across == first.astype(f32)
    leaf = jnp.broadcast_to(leaf_ref[...].astype(f32), (count, count))
    slot = jnp.broadcast_to(place, (count, count))
    tag_a = jnp.sum(jnp.where(named & (slot == 0.0), leaf, 0.0), axis=1, keepdims=True)
    tag_b = jnp.sum(jnp.where(named & (slot == 1.0), leaf, 0.0), axis=1, keepdims=True)
    tags = jnp.where(second == 0, tag_a, jnp.where(second == 1, tag_b, 0.0))
    tags_ref[...] = tags.astype(jnp.int32)
    place_ref[...] = place.astype(jnp.int32)


def requests(dests, col_leaf):
    count = dests.shape[1]
    return pl.pallas_call(
        request_kernel,
        out_shape=(
            jax.ShapeDtypeStruct((count, count), jnp.int32),
            jax.ShapeDtypeStruct((1, count), jnp.int32),
        ),
        cost_estimate=cost(1e5, 1e5),
        name="requests",
    )(dests, col_leaf)


def pack_rows(lower):
    v = [lower[8 * k : 8 * k + 8] for k in range(8)]
    row = sublanes(v[0].shape)
    moved = lambda x, lane: pltpu.roll(x, lane, 1)
    ends = pltpu.roll(v[3], 4, 0) + moved(pltpu.roll(v[3], 2, 0), 32)
    return jnp.concatenate(
        [
            v[7] + jnp.where(row < 4, moved(v[0], 60), 0.0),
            v[6] + jnp.where(row < 4, moved(v[1], 52), moved(v[0], 56)),
            v[5] + jnp.where(row < 4, moved(v[2], 44), moved(v[1], 48)),
            v[4] + jnp.where(row < 4, moved(v[3], 36), moved(v[2], 40)),
            jnp.where(row < 2, ends, 0.0),
        ],
        axis=0,
    )


def factor_kernel(
    leaves, width, source_ref, rows_ref, pack_ref, pack_up_ref, work, basis_ref, sems
):
    count, _, points = basis_ref.shape
    pieces = sems.shape[0]
    size = count // pieces
    copies = [
        pltpu.make_async_copy(
            source_ref.at[pl.ds(p * size, size)], basis_ref.at[pl.ds(p * size, size)], sems.at[p]
        )
        for p in range(pieces)
    ]
    for copy in copies:
        copy.start()
    two = 2 * width
    for q in range(0, count, 2):
        if q % size == 0:
            copies[q // size].wait()
        high, low = halves(basis_ref[q : q + 2].reshape(two, points))
        both = jnp.concatenate([high, low], axis=0).astype(bf16)
        prod = lax.dot_general(both, both, (((1,), (1,)), ((), ())), preferred_element_type=f32)
        gram = prod[:two, :two] + (prod[:two, two:] + prod[two:, :two]) + prod[two:, two:]
        work[pl.ds(q, width, stride=leaves), :] = with_identity(gram[:width])
        work[pl.ds(q + 1, width, stride=leaves), :] = with_identity(
            pltpu.roll(gram[width:], width, 1)
        )
    eliminate(work, width, leaves)
    rows_ref[...] = work[...]
    lane = lanes((two, two))
    for b in range(leaves):
        whole = work[pl.ds(b, width, stride=leaves), :]
        padded = jnp.concatenate([whole, jnp.zeros_like(whole)], axis=0)
        pack = pack_rows(jnp.where(lane < width, padded, 0.0).T[:width])
        pack_ref[b] = pack
        pack_up_ref[b] = pltpu.roll(pack, width, 1)


def leaf_factors(basis):
    leaves, width, points = basis.shape
    return pl.pallas_call(
        functools.partial(factor_kernel, leaves, width),
        in_specs=[HBM],
        out_specs=[VMEM] * 3,
        out_shape=[
            jax.ShapeDtypeStruct((width * leaves, 2 * width), f32),
            jax.ShapeDtypeStruct((leaves, 40, 2 * width), f32),
            jax.ShapeDtypeStruct((leaves, 40, 2 * width), f32),
        ],
        scratch_shapes=[
            pltpu.VMEM((width * leaves, 2 * width), f32),
            pltpu.VMEM(basis.shape, f32),
            pltpu.SemaphoreType.DMA((leaves // 8,)),
        ],
        compiler_params=pltpu.CompilerParams(vmem_limit_bytes=52 << 20),
        cost_estimate=cost(5e9, 6e6),
        name="leaf_factors",
    )(basis)


def reply_kernel(tags_ref, pack_ref, pack_up_ref, out_ref, line, table, sem):
    step = pl.program_id(0)
    count = out_ref.shape[0] // ROWS

    @pl.when(step == 0)
    def _():
        line[...] = tags_ref[...].astype(f32).T[:8].astype(jnp.int32)
        copy = pltpu.make_async_copy(line, table, sem)
        copy.start()
        copy.wait()

    for r in range(0, count, 4):
        parts = []
        for k in range(4):
            at = step * count + r + k
            part = pack_ref[table[0, at]] + pack_up_ref[table[1, at]]
            parts.append(pltpu.roll(part, 2 * k, 0) if k else part)
        base = r * ROWS
        out_ref[base : base + 32] = parts[0][:32]
        for k in range(1, 4):
            edge = base + 32 * k
            out_ref[edge : edge + 8] = parts[k - 1][32:] + parts[k][:8]
            out_ref[edge + 8 : edge + 32] = parts[k][8:32]
        out_ref[base + 128 : base + 136] = parts[3][32:]


def replies(tags, pack, pack_up):
    peers = tags.shape[0]
    leaves, rows, wide = pack.shape
    table = pl.BlockSpec((leaves, rows, wide), lambda i: (0, 0, 0))
    per = peers // 2
    return pl.pallas_call(
        reply_kernel,
        grid=(peers // per,),
        in_specs=[pl.BlockSpec(tags.shape, lambda i: (0, 0)), table, table],
        out_specs=pl.BlockSpec((per * ROWS, wide), lambda i: (i, 0)),
        out_shape=jax.ShapeDtypeStruct((peers * ROWS, wide), f32),
        scratch_shapes=[
            pltpu.VMEM((8, peers), jnp.int32),
            pltpu.SMEM((8, peers), jnp.int32),
            pltpu.SemaphoreType.DMA,
        ],
        compiler_params=ROOM,
        cost_estimate=cost(1e6, 4e6),
        name="replies",
    )(tags, pack, pack_up)


def split_rows(pair):
    width = pair.shape[1] // 2
    return jnp.concatenate([pair[:, :width], pair[:, width:]], axis=0)


def join_rows(square):
    half = square.shape[0] // 2
    return jnp.concatenate([square[:half], square[half:]], axis=1)


def pair_of(ref, n):
    return ref[pl.ds(n // 8 * 256 + n % 8, 32, stride=8), :]


def natural(pair, scratch):
    half, wide = pair.shape
    scratch[pl.ds(0, half, stride=2), :] = pair
    scratch[pl.ds(1, half, stride=2), :] = pltpu.roll(pair, wide // 2, 1)
    return scratch[:, : wide // 2]


def levels_kernel(
    work, leaf_ref, upper_ref, triple_ref, lifted_ref, one_ref, two_ref, scratch
):
    leaves, width, _ = triple_ref.shape
    two, half = 2 * width, width // 2
    target = lanes((two, width))
    source = jnp.where(target < half, 2 * target, 2 * (target - half) + 1)
    reorder = (sublanes((two, width)) == source).astype(f32).astype(bf16)
    kept = None
    for c in range(leaves // 2):
        upper = natural(pair_of(upper_ref, c), scratch.at[c])
        lifted = []
        for n in (2 * c, 2 * c + 1):
            even = work[pl.ds(n, half, stride=2 * leaves), :]
            odd = work[pl.ds(n + leaves, half, stride=2 * leaves), :]
            high, low = halves(jnp.concatenate([even, odd], axis=0))
            both = jnp.concatenate([high, low], axis=0).astype(bf16)
            moved = jnp.dot(both, reorder, preferred_element_type=f32)
            triple = jnp.concatenate(
                [moved[:width], moved[:width], moved[width:]], axis=1
            ).astype(bf16)
            triple_ref[n] = triple
            here = jnp.dot(
                triple,
                right_triple(split_rows(pair_of(leaf_ref, n))),
                preferred_element_type=f32,
            )
            lifted_ref[n] = here
            lifted.append(here)
        stack = jnp.concatenate(lifted, axis=0)
        one_ref[c] = product(stack.T, stack)
        image = product(stack, upper)
        second = product(image.T, image)
        if c % 2:
            two_ref[c // 2] = jnp.concatenate([kept, second], axis=1)
        kept = second


def levels(work, leaf_pairs, upper_pairs):
    rows, wide = work.shape
    width = wide // 2
    leaves = rows // width
    return pl.pallas_call(
        levels_kernel,
        in_specs=[VMEM] * 3,
        out_specs=[VMEM] * 4,
        out_shape=[
            jax.ShapeDtypeStruct((leaves, width, 3 * width), bf16),
            jax.ShapeDtypeStruct((leaves, width, width), f32),
            jax.ShapeDtypeStruct((leaves // 2, width, width), f32),
            jax.ShapeDtypeStruct((leaves // 4, width, wide), f32),
        ],
        scratch_shapes=[pltpu.VMEM((leaves // 2, width, wide), f32)],
        compiler_params=ROOM,
        cost_estimate=cost(5e9, 2e6),
        name="levels",
    )(work, leaf_pairs, upper_pairs)


def one_kernel(one_ref, lifted_ref, upper_ref, leaf_out, raised_out, work, scratch):
    count, width, _ = one_ref.shape
    half = width // 2
    for c in range(count):
        one = one_ref[c]
        work[pl.ds(c, width, stride=count), :] = with_identity(jnp.concatenate([one, one], axis=1))
    eliminate_small(work, width, count)
    for c in range(count):
        inverse = work[pl.ds(c, width, stride=count), :][:, width:].T
        for n in (2 * c, 2 * c + 1):
            new = product(lifted_ref[n], inverse)
            leaf_out[pl.ds(n // 8 * 256 + n % 8, half, stride=8), :] = join_rows(new)
        even = work[pl.ds(c, half, stride=2 * count), :][:, :width]
        odd = work[pl.ds(c + count, half, stride=2 * count), :][:, :width]
        raised_out[c] = product(
            jnp.concatenate([even, odd], axis=0), natural(pair_of(upper_ref, c), scratch.at[c])
        )


def level_one(one, lifted, upper_pairs):
    count, width, _ = one.shape
    return pl.pallas_call(
        one_kernel,
        in_specs=[VMEM] * 3,
        out_specs=[VMEM] * 2,
        out_shape=[
            jax.ShapeDtypeStruct((count * width, 2 * width), f32),
            jax.ShapeDtypeStruct((count, width, width), f32),
        ],
        scratch_shapes=[
            pltpu.VMEM((width * count, 2 * width), f32),
            pltpu.VMEM((count, width, 2 * width), f32),
        ],
        compiler_params=ROOM,
        cost_estimate=cost(3e9, 2e6),
        name="level_one",
    )(one, lifted, upper_pairs)


def two_kernel(own_ref, other_ref, raised_ref, upper_out, work):
    count, width, _ = raised_ref.shape
    for c in range(count):
        summed = own_ref[c // 2] + other_ref[c // 2]
        if c % 2:
            summed = pltpu.roll(summed, width, 1)
        work[pl.ds(c, width, stride=count), :] = with_identity(summed)
    eliminate_small(work, width, count)
    for c in range(count):
        inverse = work[pl.ds(c, width, stride=count), :][:, width:].T
        new = product(raised_ref[c], inverse)
        upper_out[pl.ds(c // 8 * 256 + c % 8, width // 2, stride=8), :] = join_rows(new)


def level_two(own, other, raised):
    count, width, _ = raised.shape
    return pl.pallas_call(
        two_kernel,
        in_specs=[VMEM] * 3,
        out_specs=VMEM,
        out_shape=jax.ShapeDtypeStruct((count * width // 2, 2 * width), f32),
        scratch_shapes=[pltpu.VMEM((width * count, 2 * width), f32)],
        compiler_params=ROOM,
        cost_estimate=cost(1e9, 1e6),
        name="level_two",
    )(own, other, raised)


def ortho_kernel(factor, work, basis_ref, out_ref):
    count, width, _ = basis_ref.shape
    leaves = work.shape[0] // width
    step = pl.program_id(0)
    for n in range(count):
        inverse = work[pl.ds(step * count + n, width, stride=leaves), :][:, width:]
        out_ref[n] = product(inverse * factor, basis_ref[n])


def ortho(work, basis):
    leaves, width, points = basis.shape
    part = pl.BlockSpec((leaves // 2, width, points), lambda i: (i, 0, 0))
    return pl.pallas_call(
        functools.partial(ortho_kernel, math.sqrt(points)),
        grid=(2,),
        in_specs=[VMEM, part],
        out_specs=part,
        out_shape=jax.ShapeDtypeStruct(basis.shape, f32),
        compiler_params=ROOM,
        cost_estimate=cost(5e9, 8e6),
        name="ortho",
    )(work, basis)


def left_kernel(row_ref, triple_ref, coupling_ref, first_ref, later_ref):
    size = first_ref.shape[0]

    def group(g, out_ref, start):
        for q in range(size):
            pair = []
            for i in range(2):
                at = (g * size + q) * 2 + i
                base = g * size * 64 + q // 4 * 256 + (2 * q + i) % 8
                pair.append(
                    jnp.dot(
                        triple_ref[row_ref[0, at]],
                        right_triple(split_rows(coupling_ref[pl.ds(base, 32, stride=8), :])),
                        preferred_element_type=f32,
                    )
                )
            high, low = halves(jnp.concatenate(pair, axis=1))
            out_ref[start + q] = jnp.concatenate([high, low], axis=0).astype(bf16)

    group(0, first_ref, 0)

    def later(g, _):
        group(g, later_ref, (g - 1) * size)
        return 0

    lax.fori_loop(1, 1 + later_ref.shape[0] // size, later, 0)


def lefts(row_leaf, triple, coupling_pairs):
    blocks = row_leaf.shape[1]
    wide = 2 * triple.shape[1]
    return pl.pallas_call(
        left_kernel,
        in_specs=[pl.BlockSpec(memory_space=pltpu.SMEM), VMEM, VMEM],
        out_specs=[VMEM] * 2,
        out_shape=[
            jax.ShapeDtypeStruct((blocks // 8, wide, wide), bf16),
            jax.ShapeDtypeStruct((3 * blocks // 8, wide, wide), bf16),
        ],
        compiler_params=ROOM,
        cost_estimate=cost(5e9, 6e6),
        name="lefts",
    )(row_leaf, triple, coupling_pairs)


def unpack(ref, base, place, side):
    lane, row = lanes((8, 128)) - 64 * side, sublanes((8, 128))
    shift = (place ^ side) * 64
    turn = lambda x, start: pltpu.roll(x, lax.rem(shift + (128 - start), 128), 1)
    p = [ref[pl.ds(base + 8 * k, 8), :] for k in range(4)]
    last = ref[pl.ds(base + 26, 8), :]
    middle = jnp.where(row < 6, pltpu.roll(turn(last, 0), 6, 0), turn(last, 32))
    found = [
        jnp.where(row < 4, turn(p[0], 60), turn(p[1], 56)),
        jnp.where(row < 4, turn(p[1], 52), turn(p[2], 48)),
        jnp.where(row < 4, turn(p[2], 44), turn(p[3], 40)),
        jnp.where(row < 4, turn(p[3], 36), middle),
        turn(p[3], 0),
        turn(p[2], 0),
        turn(p[1], 0),
        turn(p[0], 0),
    ]
    reach = jnp.where(row < 4, 4, 8)
    return jnp.concatenate(
        [
            jnp.where((lane >= 0) & (lane < reach + 8 * k), x, 0.0)
            for k, x in enumerate(found)
        ],
        axis=0,
    )


def finish_kernel(
    dest_ref, place_ref, first_ref, later_hbm, pack_ref, out_hbm, later_ref, out_ref, in_sems, out_sems
):
    size, wide, _ = first_ref.shape
    width = wide // 2
    lane = lanes((width // 2, wide))
    groups = out_sems.shape[0]
    rows = size * wide // 2

    def fetch(g):
        part = pl.ds((g - 1) * size, size)
        return pltpu.make_async_copy(later_hbm.at[part], later_ref.at[part], in_sems.at[g - 1])

    def put(g):
        part = pl.ds(pl.multiple_of(g * rows, rows), rows)
        return pltpu.make_async_copy(out_ref.at[part], out_hbm.at[part], out_sems.at[g])

    for g in range(1, groups):
        fetch(g).start()

    def group(g, left_ref, start):
        for q in range(size):
            lower = []
            for i in range(2):
                at = (g * size + q) * 2 + i
                lower.append(unpack(pack_ref, dest_ref[0, at] * ROWS, place_ref[0, at], i))
            high, low = halves(jnp.concatenate(lower, axis=0))
            left = left_ref[start + q]
            both = jnp.dot(left, high.astype(bf16), preferred_element_type=f32)
            done = (
                both[:width]
                + both[width:]
                + jnp.dot(left[:width], low.astype(bf16), preferred_element_type=f32)
            )
            even, odd = done[: width // 2], done[width // 2 :]
            base = g * rows + q // 4 * 256 + 2 * q % 8
            out_ref[pl.ds(base, 32, stride=8), :] = jnp.where(
                lane < width, even, pltpu.roll(odd, width, 1)
            )
            out_ref[pl.ds(base + 1, 32, stride=8), :] = jnp.where(
                lane < width, pltpu.roll(even, width, 1), odd
            )
        put(g).start()

    group(0, first_ref, 0)

    def later(g, _):
        fetch(g).wait()
        group(g, later_ref, (g - 1) * size)
        return 0

    lax.fori_loop(1, groups, later, 0)
    for g in range(groups):
        put(g).wait()


def finish(dests, place, left, packs):
    first, later = left
    size, wide, _ = first.shape
    pairs = size + later.shape[0]
    scalar = pl.BlockSpec(memory_space=pltpu.SMEM)
    shape = (pairs * wide // 2, wide)
    return pl.pallas_call(
        finish_kernel,
        in_specs=[scalar, scalar, VMEM, HBM, VMEM],
        out_specs=HBM,
        out_shape=jax.ShapeDtypeStruct(shape, f32),
        scratch_shapes=[
            pltpu.VMEM(later.shape, bf16),
            pltpu.VMEM(shape, f32),
            pltpu.SemaphoreType.DMA((pairs // size - 1,)),
            pltpu.SemaphoreType.DMA((pairs // size,)),
        ],
        compiler_params=pltpu.CompilerParams(vmem_limit_bytes=50 << 20),
        cost_estimate=cost(5e9, 8e6),
        name="finish",
    )(dests, place, first, later, packs)


def to_pairs(rows):
    count, square = rows.shape
    tiles = rows.reshape(count // 8, 8, square // 128, 128).transpose(0, 2, 1, 3)
    return tiles.reshape(count * square // 128, 128)


def from_pairs(pairs, square):
    count = pairs.shape[0] * 128 // square
    tiles = pairs.reshape(count // 8, square // 128, 8, 128).transpose(0, 2, 1, 3)
    return tiles.reshape(count, square)


def shards(basis, leaf_transfer, upper_transfer, coupling, row_leaf, col_dev, col_leaf):
    blocks, square = coupling.shape
    dests = col_dev.reshape(1, blocks)
    tags, place = requests(dests, col_leaf.reshape(1, blocks))
    asked = lax.all_to_all(tags, BOTH, split_axis=0, concat_axis=0, tiled=True)
    work, pack, pack_up = leaf_factors(basis)
    answers = replies(asked, pack, pack_up).reshape(asked.shape[0], 1, -1)
    packs = lax.all_to_all(answers, BOTH, split_axis=0, concat_axis=0, tiled=True)
    packs = packs.reshape(-1, pack.shape[2])
    upper_pairs = to_pairs(upper_transfer)
    triple, lifted, one, own = levels(work, to_pairs(leaf_transfer), upper_pairs)
    size = lax.axis_size("grp")
    other = lax.ppermute(own, "grp", [(i, i ^ 1) for i in range(size)])
    left = lefts(row_leaf.reshape(1, blocks), triple, to_pairs(coupling))
    ortho_basis = ortho(work, basis)
    leaf_out, raised = level_one(one, lifted, upper_pairs)
    upper_out = level_two(own, other, raised)
    coupling_out = finish(dests, place, left, packs)
    return (
        ortho_basis,
        from_pairs(leaf_out, square),
        from_pairs(upper_out, square),
        from_pairs(coupling_out, square),
    )


def solution(mesh):
    both = P(BOTH, None)
    in_specs = (P(BOTH, None, None), both, both, both, P(BOTH), both, P(BOTH))
    out_specs = (P(BOTH, None, None), both, both, both)
    return jax.shard_map(shards, mesh=mesh, in_specs=in_specs, out_specs=out_specs, check_vma=False)
```
